32 devices in a mesh: row: 8 (over y, x, core), col: 4 (over z).
Axes of the slice: x: 2, y: 2, z: 4, core: 2. Of those that a mesh axis runs over, the one named last changes fastest.
Arguments:
- inputs: bfloat16 [1024, 5120], P('row', 'col'), may hold values from -6 to 6
- grad_out: bfloat16 [1024, 5120], P('row', 'col'), may hold values from -6 to 6
- pre_act: bfloat16 [1024, 13824], P('col', 'row'), may hold values from -6 to 6
- w_in: bfloat16 [13824, 5120], P('row', 'col'), may hold values from -0.078125 to 0.078125
- w_out: bfloat16 [13824, 5120], P('row', 'col'), may hold values from -0.0546875 to 0.0546875
- row_in_prev: float32 [13824], P('row'), may hold values from 51.2 to 6144, as said below
- col_in_prev: float32 [5120], P('col'), may hold values from 51.2 to 6144, as said below
- row_out_prev: float32 [13824], P('row'), may hold values from 51.2 to 6144, as said below
- col_out_prev: float32 [5120], P('col'), may hold values from 51.2 to 6144, as said below
Outputs:
- input_grad: bfloat16 [1024, 5120], P('row', 'col')
- update_in: float32 [13824, 5120], P('row', 'col')
- row_in: float32 [13824], P('row')
- col_in: float32 [5120], P('col')
- update_out: float32 [13824, 5120], P('row', 'col')
- row_out: float32 [13824], P('row')
- col_out: float32 [5120], P('col')
The draws below stay inside these ranges and needn't reach their ends.
Inputs may be any that keep to these rules, and one draw needn't show every extreme that they name: `row_in_prev`: positive. `col_in_prev`: positive. `row_out_prev`: positive. `col_out_prev`: positive.
All inputs are finite; a program needn't handle non-finite values.
Results may differ from the reference program's by a relative error of at most 0.023.
Values may be sent and summed in bfloat16 or wider, within the bound.
No kernel may reach another device: no remote copies, remote signals or barrier semaphores. Data moves between devices by JAX's collectives and lax.ppermute only.
A program may use at most 128 MiB of HBM per device.

```python
import math
import jax
import jax.numpy as jnp
from jax import lax

D = 5120
FF = 13824
TOKENS = 1024
N_ROW = 8


def falling_moments(key, salt, length):
    key = jax.random.fold_in(key, salt)
    position = jnp.arange(length).astype(jnp.float32) / length
    spread = jax.random.uniform(key, (length,), jnp.float32, jnp.log(0.5), jnp.log(2.0))
    factor = 10.0
    return TOKENS * jnp.exp(spread) * 3.0 * jnp.exp(-jnp.log(factor) * position)


def draw_row_in_prev(key, part):
    return falling_moments(key, 11, FF)


def draw_col_in_prev(key, part):
    return falling_moments(key, 23, D)


def draw_row_out_prev(key, part):
    return falling_moments(key, 37, FF)


def draw_col_out_prev(key, part):
    return falling_moments(key, 41, D)


def levels(stream_key, extent, split, least, largest):
    def one(axis_at, parts):
        heights = jax.random.uniform(jax.random.fold_in(jax.random.fold_in(stream_key, 6), axis_at), (parts,), jnp.float32, least / len(split), largest / len(split))
        return jnp.repeat(jnp.exp(heights), extent[axis_at] // parts).reshape((-1,) + (1,) * (len(extent) - axis_at - 1))

    gain = one(*split[0])
    for cut in split[1:]:
        gain = gain * one(*cut)
    return gain


def gaussian(rng, dims, scale, reach, cuts=(), kind=jnp.bfloat16):
    result = jax.random.normal(rng, dims, jnp.float32) * scale
    if len(cuts) > 0:
        result = levels(rng, dims, cuts, -0.22, 0.18) * result
    return jnp.clip(result, min=-reach, max=reach).astype(kind)


def setup_inputs(seed: int = 0) -> dict:
    seeds = jax.random.split(jax.random.key(seed), 10)
    inputs = gaussian(seeds[0], (TOKENS, D), 1.0, 6.0, ((0, 8), (1, 4)))
    grad_out = gaussian(seeds[1], (TOKENS, D), 1.0, 6.0, ((0, 8), (1, 4)))
    pre_act = gaussian(seeds[2], (TOKENS, FF), 1.0, 6.0, ((0, 4), (1, 8)))
    w_in = gaussian(seeds[3], (FF, D), D ** -0.5, 0.078125, ((0, 8), (1, 4)))
    w_out = gaussian(seeds[4], (FF, D), FF ** -0.5, 0.0546875, ((0, 8), (1, 4)))
    row_in_prev = draw_row_in_prev(jax.random.fold_in(seeds[9], 71), 0)
    col_in_prev = draw_col_in_prev(jax.random.fold_in(seeds[9], 71), 0)
    row_out_prev = draw_row_out_prev(jax.random.fold_in(seeds[9], 71), 0)
    col_out_prev = draw_col_out_prev(jax.random.fold_in(seeds[9], 71), 0)
    return {"inputs": inputs, "grad_out": grad_out, "pre_act": pre_act, "w_in": w_in, "w_out": w_out, "row_in_prev": row_in_prev, "col_in_prev": col_in_prev, "row_out_prev": row_out_prev, "col_out_prev": col_out_prev}


decay_rate = 0.8
epsilon_sq = 1e-30
clip_limit = 0.25
gelu_coef = 0.044715
root_coef = math.sqrt(2.0 / math.pi)

def gelu_parts(pre_float):
    tanh_value = jnp.tanh(root_coef * (pre_float + gelu_coef * pre_float * pre_float * pre_float))
    value = 0.5 * pre_float * (1.0 + tanh_value)
    slope = 0.5 * (1.0 + tanh_value) + 0.5 * pre_float * (1.0 - tanh_value * tanh_value) * root_coef * (1.0 + 3.0 * gelu_coef * pre_float * pre_float)
    return (value, slope)

def adafactor(gradient, row_prev, col_prev):
    square = gradient * gradient
    row_next = decay_rate * row_prev + (1.0 - decay_rate) * (lax.optimization_barrier(jnp.sum(square, axis=1)) / D + epsilon_sq)
    col_next = decay_rate * col_prev + (1.0 - decay_rate) * (lax.optimization_barrier(jnp.sum(square, axis=0)) / FF + epsilon_sq)
    raw = gradient / jnp.sqrt(row_next[:, None] * col_next[None, :] / TOKENS)
    rms_value = jnp.sqrt(jnp.sum(raw * raw) / (FF * D))
    return (raw / jnp.maximum(1.0, rms_value / clip_limit), row_next, col_next)

def reference(inputs, grad_out, pre_act, w_in, w_out, row_in_prev, col_in_prev, row_out_prev, col_out_prev):
    value, slope = gelu_parts(pre_act.astype(jnp.float32))
    act = value.astype(jnp.bfloat16)
    hidden_grad = jnp.dot(grad_out, w_out.T, preferred_element_type=jnp.float32)
    pre_grad = (hidden_grad * slope).astype(jnp.bfloat16)
    grad_w_out = jnp.dot(act.T, grad_out, preferred_element_type=jnp.float32)
    grad_w_in = jnp.dot(pre_grad.T, inputs, preferred_element_type=jnp.float32)
    block_rows = FF // N_ROW
    hidden_blocks = pre_grad.reshape(TOKENS, N_ROW, block_rows).transpose(1, 0, 2)
    weight_blocks = w_in.reshape(N_ROW, block_rows, D)

    def add_block(total, pair):
        term = jnp.dot(pair[0], pair[1], preferred_element_type=jnp.float32).astype(jnp.bfloat16)
        term = lax.optimization_barrier(term)
        return (total + term.astype(jnp.float32), None)
    summed, _ = lax.scan(add_block, jnp.zeros((TOKENS, D), jnp.float32), (hidden_blocks, weight_blocks))
    input_grad = summed.astype(jnp.bfloat16)
    update_in, row_in, col_in = adafactor(grad_w_in, row_in_prev, col_in_prev)
    update_out, row_out, col_out = adafactor(grad_w_out, row_out_prev, col_out_prev)
    return (input_grad, update_in, row_in, col_in, update_out, row_out, col_out)
```

```python
import functools
import math

import jax
import jax.numpy as jnp
from jax import lax
from jax.experimental import pallas as pl
from jax.experimental.pallas import tpu as pltpu
from jax.sharding import PartitionSpec as P


D = 5120
FF = 13824

decay_rate = 0.8
epsilon_sq = 1e-30
clip_limit = 0.25
gelu_coef = 0.044715
root_coef = math.sqrt(2.0 / math.pi)

bf16 = jnp.bfloat16
f32 = jnp.float32


def gelu_parts(pre_float):
    tanh_value = jnp.tanh(root_coef * (pre_float + gelu_coef * pre_float * pre_float * pre_float))
    value = 0.5 * pre_float * (1.0 + tanh_value)
    slope = 0.5 * (1.0 + tanh_value) + 0.5 * pre_float * (
        1.0 - tanh_value * tanh_value
    ) * root_coef * (1.0 + 3.0 * gelu_coef * pre_float * pre_float)
    return (value, slope)


def row_moment(row_sum, row_prev):
    return decay_rate * row_prev + (1.0 - decay_rate) * (row_sum / D + epsilon_sq)


def col_moment(col_sum, col_prev):
    return decay_rate * col_prev + (1.0 - decay_rate) * (col_sum / FF + epsilon_sq)


def swap(x, axis, bit):
    n = lax.axis_size(axis)
    return lax.ppermute(x, axis, [(i, i ^ bit) for i in range(n)])


def total(x, axis):
    bit = 1
    while bit < lax.axis_size(axis):
        x = x + swap(x, axis, bit)
        bit *= 2
    return x


def line_gather(x, axis):
    n = lax.axis_size(axis)
    low, high = [], []
    up = down = x
    for k in range(1, n):
        up = lax.ppermute(up, axis, [(i, i + 1) for i in range(k - 1, n - 1)])
        down = lax.ppermute(down, axis, [(i, i - 1) for i in range(1, n - k + 1)])
        low.append(up)
        high.append(down)
    return low, high


def line_scatter_sum(where, parts, up, down, axis, unit):
    n = lax.axis_size(axis)
    for k in range(1, n):
        up = lax.ppermute(up, axis, [(i, i + 1) for i in range(min(k, n - 1))])
        down = lax.ppermute(down, axis, [(i, i - 1) for i in range(max(n - k, 1), n)])
        if k < n - 1:
            up, down = add_parts(where, parts, up, down, n - k - 1, unit)
    return up, down


def split_bits(offset):
    return 1 << (offset.bit_length() - 1), offset & -offset


def block_gather(x):
    count = lax.axis_size("row")
    half = x.shape[0] // 2
    got = {0: x}
    for offset in sorted(range(2, count, 2), key=lambda o: bin(o).count("1")):
        high, low = split_bits(offset)
        if high == low:
            got[offset] = swap(x, "row", high)
        else:
            first = swap(got[offset - high][:half], "row", high)
            second = swap(got[offset - low][half:], "row", low)
            got[offset] = jnp.concatenate([first, second], axis=0)
    for offset in range(0, count, 2):
        got[offset + 1] = swap(got[offset], "row", 1)
    return [got[o] for o in range(count)]


def block_scatter_sum(y):
    count = lax.axis_size("row")
    here = lax.axis_index("row")
    chips = count // 2
    block = y.shape[0] // count
    y = y.reshape(chips, 2, block, y.shape[1])
    core = here % 2
    chip = here // 2
    mine = lax.dynamic_index_in_dim(y, core, 1, keepdims=False)
    other = lax.dynamic_index_in_dim(y, 1 - core, 1, keepdims=False)
    both = mine.astype(f32) + swap(other, "row", 1).astype(f32)
    both = both.astype(bf16)
    half = block // 2

    def piece(offset, start, size):
        return lax.dynamic_slice(both, (chip ^ offset, start, 0), (1, size, y.shape[3]))[0]

    first = {o: piece(o, 0, half) for o in range(chips)}
    second = {o: piece(o, half, half) for o in range(chips)}
    for offset in sorted(range(1, chips), key=lambda o: -bin(o).count("1")):
        high, low = split_bits(offset)
        if high == low:
            whole = jnp.concatenate([first[offset], second[offset]], axis=0)
            whole = swap(whole, "row", 2 * high)
            first[0] = first[0].astype(f32) + whole[:half].astype(f32)
            second[0] = second[0].astype(f32) + whole[half:].astype(f32)
        else:
            a = swap(first[offset], "row", 2 * high)
            b = swap(second[offset], "row", 2 * low)
            first[offset - high] = first[offset - high] + a
            second[offset - low] = second[offset - low] + b
    return jnp.concatenate([first[0], second[0]], axis=0).astype(bf16)


def unit_of(hidden):
    return max(u for u in range(16, 321, 16) if hidden % u == 0)


def gelu_kernel(pre_ref, act_ref, slope_ref):
    value, slope = gelu_parts(pre_ref[...].astype(f32))
    act_ref[...] = value.astype(bf16)
    slope_ref[...] = slope


def gelu(pre_t, unit, first, units):
    tokens = pre_t.shape[1]
    shape = (units * unit, tokens)
    block = pl.BlockSpec((unit, tokens), lambda i: (i, 0))
    return pl.pallas_call(
        gelu_kernel,
        out_shape=(jax.ShapeDtypeStruct(shape, bf16), jax.ShapeDtypeStruct(shape, f32)),
        grid=(units,),
        in_specs=[pl.BlockSpec((unit, tokens), lambda i: (i + first, 0))],
        out_specs=(block, block),
        name="gelu",
    )(pre_t)


def whole(shape):
    zeros = (0,) * len(shape)
    return pl.BlockSpec(shape, lambda *_: zeros)


def assemble_body(where, pieces, out_ref):
    block = pieces[0].shape[0]
    for o, piece in enumerate(pieces):
        start = pl.multiple_of((where[1] ^ o) * block, block)
        out_ref[pl.ds(start, block), :] = piece[...]


def assemble_kernel(where, *refs):
    assemble_body(where, refs[:-1], refs[-1])


def assemble(where, pieces):
    count = len(pieces)
    block, width = pieces[0].shape
    shape = (count * block, width)
    return pl.pallas_call(
        assemble_kernel,
        out_shape=jax.ShapeDtypeStruct(shape, bf16),
        grid_spec=pltpu.PrefetchScalarGridSpec(
            num_scalar_prefetch=1,
            grid=(1,),
            in_specs=[whole((block, width))] * count,
            out_specs=whole(shape),
        ),
        name="assemble",
    )(where, *pieces)


def hidden_kernel(where, *refs, pieces):
    g_refs, (w_ref, out_ref, last_ref, first_ref) = refs[: max(pieces, 1)], refs[max(pieces, 1) :][:4]
    if pieces:
        g_ref = refs[pieces + 4]

        @pl.when(pl.program_id(0) == 0)
        def _():
            assemble_body(where, g_refs, g_ref)
    else:
        g_ref = g_refs[0]
    n, _, tokens = out_ref.shape
    w = w_ref[...]
    for j in range(n):
        result = lax.dot_general(
            w,
            g_ref[pl.ds(j * tokens, tokens), :],
            (((1,), (1,)), ((), ())),
            preferred_element_type=f32,
        ).astype(bf16)
        out_ref[j] = result
        if j == 0:
            first_ref[...] = result
        if j == n - 1:
            last_ref[...] = result


def hidden_partial(where, w_out, grads, n, unit, first, units):
    pieces = len(grads) if len(grads) > 1 else 0
    tokens = sum(g.shape[0] for g in grads)
    width = w_out.shape[1]
    shape = (units * unit, tokens // n)
    part = pl.BlockSpec((unit, tokens // n), lambda i, w: (i, 0))
    return pl.pallas_call(
        functools.partial(hidden_kernel, pieces=pieces),
        out_shape=(
            jax.ShapeDtypeStruct((n,) + shape, bf16),
            jax.ShapeDtypeStruct(shape, bf16),
            jax.ShapeDtypeStruct(shape, bf16),
        )
        + ((jax.ShapeDtypeStruct((tokens, width), bf16),) if pieces else ()),
        grid_spec=pltpu.PrefetchScalarGridSpec(
            num_scalar_prefetch=1,
            grid=(units,),
            in_specs=[whole(g.shape) for g in grads]
            + [pl.BlockSpec((unit, width), lambda i, w: (i + first, 0))],
            out_specs=(
                pl.BlockSpec((n, unit, tokens // n), lambda i, w: (0, i, 0)),
                part,
                part,
            )
            + ((whole((tokens, width)),) if pieces else ()),
        ),
        name="hidden_partial",
    )(where, *grads, w_out)


def add_kernel(where, low_ref, high_ref, up_ref, down_ref, up_out, down_out):
    up_out[...] = (low_ref[0].astype(f32) + up_ref[...].astype(f32)).astype(bf16)
    down_out[...] = (high_ref[0].astype(f32) + down_ref[...].astype(f32)).astype(bf16)


def add_parts(where, parts, up, down, hops, unit):
    n, hidden, tokens = parts.shape
    block = pl.BlockSpec((unit, tokens), lambda i, w: (i, 0))
    return pl.pallas_call(
        add_kernel,
        out_shape=(jax.ShapeDtypeStruct(up.shape, bf16),) * 2,
        grid_spec=pltpu.PrefetchScalarGridSpec(
            num_scalar_prefetch=1,
            grid=(hidden // unit,),
            in_specs=[
                pl.BlockSpec((1, unit, tokens), lambda i, w: (jnp.minimum(w[0] + hops, n - 1), i, 0)),
                pl.BlockSpec((1, unit, tokens), lambda i, w: (jnp.maximum(w[0] - hops, 0), i, 0)),
                block,
                block,
            ],
            out_specs=(block, block),
        ),
        name="add_parts",
    )(where, parts, parts, up, down)


def own_kernel(where, part_ref, up_ref, down_ref, slope_ref, out_ref):
    total_grad = part_ref[0].astype(f32) + up_ref[...].astype(f32) + down_ref[...].astype(f32)
    out_ref[...] = (total_grad * slope_ref[...]).astype(bf16)


def own_grad(where, parts, up, down, slope, unit):
    _, hidden, tokens = parts.shape
    block = pl.BlockSpec((unit, tokens), lambda i, w: (i, 0))
    return pl.pallas_call(
        own_kernel,
        out_shape=jax.ShapeDtypeStruct(up.shape, bf16),
        grid_spec=pltpu.PrefetchScalarGridSpec(
            num_scalar_prefetch=1,
            grid=(hidden // unit,),
            in_specs=[
                pl.BlockSpec((1, unit, tokens), lambda i, w: (w[0], i, 0)),
                block,
                block,
                block,
            ],
            out_specs=block,
        ),
        name="own_grad",
    )(where, parts, up, down, slope)


def fetch(where, refs, buffer, sems):
    n = (len(refs) + 1) // 2
    tokens = refs[0].shape[1]
    for here in range(n):

        @pl.when(where[0] == here)
        def _():
            for j in range(n):
                source = refs[0] if j == here else refs[here - j] if j < here else refs[n - 1 + j - here]
                pltpu.make_async_copy(
                    source, buffer.at[:, pl.ds(j * tokens, tokens)], sems.at[j]
                ).start()

    for j in range(n):
        pltpu.make_async_copy(
            refs[0], buffer.at[:, pl.ds(j * tokens, tokens)], sems.at[j]
        ).wait()


def weight_kernel(where, *refs, n):
    pieces, x_ref = refs[: 2 * n - 1], refs[2 * n - 1]
    out_ref, row_ref, col_ref, buffer, sems = refs[-5:]
    step = pl.program_id(0)
    unit = out_ref.shape[0]

    @pl.when(step == 0)
    def _():
        fetch(where, pieces, buffer, sems)
        col_ref[...] = jnp.zeros_like(col_ref)

    start = pl.multiple_of(step * unit, unit)
    acc = jnp.dot(buffer[pl.ds(start, unit), :], x_ref[...], preferred_element_type=f32)
    out_ref[...] = acc
    square = acc * acc
    row_ref[...] = jnp.sum(square, axis=1)[None, None, :]
    col_ref[...] += jnp.sum(square.reshape(unit // 8, 8, square.shape[1]), axis=0)


def weight_grad(where, own, low, high, x_all, unit, first, hidden, before):
    size, tokens = own.shape
    n = len(low) + 1
    units = size // unit
    width = x_all.shape[1]
    grad, rows, cols = pl.pallas_call(
        functools.partial(weight_kernel, n=n),
        out_shape=(
            jax.ShapeDtypeStruct((hidden, width), f32),
            jax.ShapeDtypeStruct((units, 1, unit), f32),
            jax.ShapeDtypeStruct((8, width), f32),
        ),
        grid_spec=pltpu.PrefetchScalarGridSpec(
            num_scalar_prefetch=1,
            grid=(units,),
            in_specs=[pl.BlockSpec(memory_space=pl.ANY)] * (2 * n - 1)
            + [whole((n * tokens, width))]
            + ([] if before is None else [pl.BlockSpec(memory_space=pl.ANY)]),
            out_specs=(
                pl.BlockSpec((unit, width), lambda i, w: (i + first, 0)),
                pl.BlockSpec((1, 1, unit), lambda i, w: (i, 0, 0)),
                pl.BlockSpec((8, width), lambda i, w: (0, 0)),
            ),
            scratch_shapes=[
                pltpu.VMEM((size, n * tokens), bf16),
                pltpu.SemaphoreType.DMA((n,)),
            ],
        ),
        input_output_aliases={} if before is None else {2 * n + 1: 0},
        name="weight_grad",
    )(where, own, *low, *high, x_all, *([] if before is None else [before]))
    return grad, rows.reshape(size), jnp.sum(cols, axis=0)


def input_kernel(where, *refs, n, has_prev):
    pieces, w_ref = refs[: 2 * n - 1], refs[2 * n - 1]
    out_ref, buffer, sems = refs[-3:]
    step = pl.program_id(0)
    tokens = out_ref.shape[0]

    @pl.when(step == 0)
    def _():
        fetch(where, pieces, buffer, sems)

    start = pl.multiple_of(step * tokens, tokens)
    acc = lax.dot_general(
        buffer[:, pl.ds(start, tokens)],
        w_ref[...],
        (((0,), (0,)), ((), ())),
        preferred_element_type=f32,
    )
    if has_prev:
        acc = acc + refs[2 * n][...]
    out_ref[...] = acc.astype(out_ref.dtype)


def input_partial(where, own, low, high, w_part, prev, out_dtype):
    hidden, tokens = own.shape
    n = len(low) + 1
    width = w_part.shape[1]
    row = pl.BlockSpec((tokens, width), lambda i, w: (i, 0))
    return pl.pallas_call(
        functools.partial(input_kernel, n=n, has_prev=prev is not None),
        out_shape=jax.ShapeDtypeStruct((n * tokens, width), out_dtype),
        grid_spec=pltpu.PrefetchScalarGridSpec(
            num_scalar_prefetch=1,
            grid=(n,),
            in_specs=[pl.BlockSpec(memory_space=pl.ANY)] * (2 * n - 1)
            + [whole((hidden, width))]
            + ([] if prev is None else [row]),
            out_specs=row,
            scratch_shapes=[
                pltpu.VMEM((hidden, n * tokens), bf16),
                pltpu.SemaphoreType.DMA((n,)),
            ],
        ),
        name="input_partial",
    )(where, own, *low, *high, w_part, *([] if prev is None else [prev]))


PARTS = 2


def spans(units, parts):
    cuts = [units * p // parts for p in range(parts + 1)]
    return [(a, b) for a, b in zip(cuts, cuts[1:]) if b > a]


def step(
    inputs, grad_out, pre_act, w_in, w_out, row_in_prev, col_in_prev, row_out_prev, col_out_prev
):
    n = lax.axis_size("col")
    here = lax.axis_index("col")
    where = jnp.stack([here, lax.axis_index("row")]).astype(jnp.int32)
    token_count = float(inputs.shape[0] * lax.axis_size("row"))
    hidden = w_in.shape[0]
    unit = unit_of(hidden)
    units = hidden // unit
    pre_t = pre_act.T
    cuts = spans(units, PARTS)

    acts, slopes = [], []
    for a, b in cuts:
        own, slope = gelu(pre_t, unit, a, b - a)
        acts.append((own,) + line_gather(own, "col"))
        slopes.append(slope)

    grads = block_gather(grad_out)
    all_parts = []
    for a, b in cuts:
        made = hidden_partial(where, w_out, grads, n, unit, a, b - a)
        if len(made) == 4:
            grads = [made[3]]
        all_parts.append(made[:3])
    grad_all = grads[0]
    input_all = assemble(where, block_gather(inputs))

    grad_in, rows_in, cols_in = None, [], 0.0
    partial = None
    for p, (a, b) in enumerate(cuts):
        parts, last, first = all_parts[p]
        up, down = line_scatter_sum(where, parts, last, first, "col", unit)
        own = own_grad(where, parts, up, down, slopes[p], unit)
        low, high = line_gather(own, "col")
        final = p == len(cuts) - 1
        partial = input_partial(
            where, own, low, high, w_in[a * unit : b * unit], partial, bf16 if final else f32
        )
        grad_in, rows, cols = weight_grad(
            where, own, low, high, input_all, unit, a, hidden, grad_in
        )
        rows_in.append(rows)
        cols_in = cols_in + cols

    grad_o, rows_out, cols_out = None, [], 0.0
    for p, (a, b) in enumerate(cuts):
        own, low, high = acts[p]
        grad_o, rows, cols = weight_grad(where, own, low, high, grad_all, unit, a, hidden, grad_o)
        rows_out.append(rows)
        cols_out = cols_out + cols

    input_grad = block_scatter_sum(partial)

    def finish(gradient, rows, cols, row_prev, col_prev):
        row_next = row_moment(total(jnp.concatenate(rows), "col"), row_prev)
        weighted = jnp.sum(gradient * gradient / row_next[:, None], axis=0)
        cols, weighted = total(jnp.stack([cols, weighted]), "row")
        col_next = col_moment(cols, col_prev)
        norm = total(jnp.sum(weighted / col_next)[None], "col")[0]
        rms_value = jnp.sqrt(token_count * norm / (FF * D))
        divisor = jnp.maximum(1.0, rms_value / clip_limit)
        raw = gradient / jnp.sqrt(row_next[:, None] * col_next[None, :] / token_count)
        return raw / divisor, row_next, col_next

    update_out, row_out, col_out = finish(grad_o, rows_out, cols_out, row_out_prev, col_out_prev)
    update_in, row_in, col_in = finish(grad_in, rows_in, cols_in, row_in_prev, col_in_prev)
    return (input_grad, update_in, row_in, col_in, update_out, row_out, col_out)


def solution(mesh):
    return jax.shard_map(
        step,
        mesh=mesh,
        in_specs=(
            P("row", "col"),
            P("row", "col"),
            P("col", "row"),
            P("row", "col"),
            P("row", "col"),
            P("row"),
            P("col"),
            P("row"),
            P("col"),
        ),
        out_specs=(
            P("row", "col"),
            P("row", "col"),
            P("row"),
            P("col"),
            P("row", "col"),
            P("row"),
            P("col"),
        ),
        check_vma=False,
    )
```

```python
import functools
import math

import jax
import jax.numpy as jnp
from jax import lax
from jax.experimental import pallas as pl
from jax.experimental.pallas import tpu as pltpu
from jax.sharding import PartitionSpec as P


D = 5120
FF = 13824

decay_rate = 0.8
epsilon_sq = 1e-30
clip_limit = 0.25
gelu_coef = 0.044715
root_coef = math.sqrt(2.0 / math.pi)

bf16 = jnp.bfloat16
f32 = jnp.float32


def gelu_parts(pre_float):
    tanh_value = jnp.tanh(root_coef * (pre_float + gelu_coef * pre_float * pre_float * pre_float))
    value = 0.5 * pre_float * (1.0 + tanh_value)
    slope = 0.5 * (1.0 + tanh_value) + 0.5 * pre_float * (
        1.0 - tanh_value * tanh_value
    ) * root_coef * (1.0 + 3.0 * gelu_coef * pre_float * pre_float)
    return (value, slope)


def row_moment(row_sum, row_prev):
    return decay_rate * row_prev + (1.0 - decay_rate) * (row_sum / D + epsilon_sq)


def col_moment(col_sum, col_prev):
    return decay_rate * col_prev + (1.0 - decay_rate) * (col_sum / FF + epsilon_sq)


def swap(x, axis, bit):
    n = lax.axis_size(axis)
    return lax.ppermute(x, axis, [(i, i ^ bit) for i in range(n)])


def total(x, axis):
    n = lax.axis_size(axis)
    if n == 4:
        one, two, three = (swap(x, axis, bit) for bit in (1, 2, 3))
        return (x + one) + (two + three)
    bit = 1
    while bit < n:
        x = x + swap(x, axis, bit)
        bit *= 2
    return x


def line_gather(x, axis):
    n = lax.axis_size(axis)
    low, high = [], []
    up = down = x
    for k in range(1, n):
        up = lax.ppermute(up, axis, [(i, i + 1) for i in range(k - 1, n - 1)])
        down = lax.ppermute(down, axis, [(i, i - 1) for i in range(1, n - k + 1)])
        low.append(up)
        high.append(down)
    return low, high


def line_scatter_sum(parts, up, down, axis):
    n = lax.axis_size(axis)
    here = lax.axis_index(axis)

    def part(index):
        return lax.dynamic_index_in_dim(parts, index, 0, keepdims=False)

    for k in range(1, n):
        up = lax.ppermute(up, axis, [(i, i + 1) for i in range(min(k, n - 1))])
        down = lax.ppermute(down, axis, [(i, i - 1) for i in range(max(n - k, 1), n)])
        if k < n - 1:
            up = up + part(jnp.minimum(here + n - k - 1, n - 1))
            down = down + part(jnp.maximum(here - (n - k - 1), 0))
    return up, down


def split_bits(offset):
    return 1 << (offset.bit_length() - 1), offset & -offset


def block_gather(x):
    count = lax.axis_size("row")
    half = x.shape[0] // 2
    got = {0: x}
    for offset in sorted(range(2, count, 2), key=lambda o: bin(o).count("1")):
        high, low = split_bits(offset)
        if high == low:
            got[offset] = swap(x, "row", high)
        else:
            first = swap(got[offset - high][:half], "row", high)
            second = swap(got[offset - low][half:], "row", low)
            got[offset] = jnp.concatenate([first, second], axis=0)
    for offset in range(0, count, 2):
        got[offset + 1] = swap(got[offset], "row", 1)
    return [got[o] for o in range(count)]


def block_scatter_sum(mine, other):
    chips = mine.shape[0]
    half = mine.shape[1] // 2
    arrived = swap(other, "row", 1)
    both = [
        (mine[o].astype(f32) + arrived[o].astype(f32)).astype(bf16) for o in range(chips)
    ]
    first = [v[:half] for v in both]
    second = [v[half:] for v in both]
    moved = both[:1]
    for offset in sorted(range(1, chips), key=lambda o: -bin(o).count("1")):
        high, low = split_bits(offset)
        if high == low:
            piece = jnp.concatenate([first[offset], second[offset]], axis=0)
            moved.append(swap(piece, "row", 2 * high))
        else:
            a = swap(first[offset], "row", 2 * high)
            b = swap(second[offset], "row", 2 * low)
            first[offset - high] = first[offset - high] + a
            second[offset - low] = second[offset - low] + b
    return sum(v.astype(f32) for v in moved).astype(bf16)


def unit_of(hidden):
    return max(u for u in range(16, 321, 16) if hidden % u == 0)


def gelu_kernel(pre_ref, act_ref, slope_ref):
    value, slope = gelu_parts(pre_ref[...].astype(f32))
    act_ref[...] = value.astype(bf16)
    slope_ref[...] = slope


def gelu(pre_t, unit, first, units):
    tokens = pre_t.shape[1]
    shape = (units * unit, tokens)
    block = pl.BlockSpec((unit, tokens), lambda i: (i, 0))
    return pl.pallas_call(
        gelu_kernel,
        out_shape=(jax.ShapeDtypeStruct(shape, bf16), jax.ShapeDtypeStruct(shape, f32)),
        grid=(units,),
        in_specs=[pl.BlockSpec((unit, tokens), lambda i: (i + first, 0))],
        out_specs=(block, block),
        name="gelu",
    )(pre_t)


def whole(shape):
    zeros = (0,) * len(shape)
    return pl.BlockSpec(shape, lambda *_: zeros)


def assemble_body(where, pieces, out_ref):
    block = pieces[0].shape[0]
    for o, piece in enumerate(pieces):
        start = pl.multiple_of((where[1] ^ o) * block, block)
        out_ref[pl.ds(start, block), :] = piece[...]


def hidden_kernel(where, *refs, pieces):
    g_refs, (w_ref, out_ref, last_ref, first_ref) = refs[: max(pieces, 1)], refs[max(pieces, 1) :][:4]
    if pieces:
        g_ref = refs[pieces + 4]

        @pl.when(pl.program_id(0) == 0)
        def _():
            assemble_body(where, g_refs, g_ref)
    else:
        g_ref = g_refs[0]
    n, _, tokens = out_ref.shape
    w = w_ref[...]
    for j in range(n):
        result = lax.dot_general(
            w,
            g_ref[pl.ds(j * tokens, tokens), :],
            (((1,), (1,)), ((), ())),
            preferred_element_type=f32,
        ).astype(bf16)
        out_ref[j] = result
        if j == 0:
            first_ref[...] = result
        if j == n - 1:
            last_ref[...] = result


def hidden_partial(where, w_out, grads, n, unit, first, units):
    pieces = len(grads) if len(grads) > 1 else 0
    tokens = sum(g.shape[0] for g in grads)
    width = w_out.shape[1]
    shape = (units * unit, tokens // n)
    part = pl.BlockSpec((unit, tokens // n), lambda i, w: (i, 0))
    return pl.pallas_call(
        functools.partial(hidden_kernel, pieces=pieces),
        out_shape=(
            jax.ShapeDtypeStruct((n,) + shape, bf16),
            jax.ShapeDtypeStruct(shape, bf16),
            jax.ShapeDtypeStruct(shape, bf16),
        )
        + ((jax.ShapeDtypeStruct((tokens, width), bf16),) if pieces else ()),
        grid_spec=pltpu.PrefetchScalarGridSpec(
            num_scalar_prefetch=1,
            grid=(units,),
            in_specs=[whole(g.shape) for g in grads]
            + [pl.BlockSpec((unit, width), lambda i, w: (i + first, 0))],
            out_specs=(
                pl.BlockSpec((n, unit, tokens // n), lambda i, w: (0, i, 0)),
                part,
                part,
            )
            + ((whole((tokens, width)),) if pieces else ()),
        ),
        name="hidden_partial",
    )(where, *grads, w_out)


def fetch(where, refs, buffer, sems):
    n = (len(refs) + 1) // 2
    tokens = refs[0].shape[1]
    for here in range(n):

        @pl.when(where[0] == here)
        def _():
            for j in range(n):
                source = refs[0] if j == here else refs[here - j] if j < here else refs[n - 1 + j - here]
                pltpu.make_async_copy(
                    source, buffer.at[:, pl.ds(j * tokens, tokens)], sems.at[j]
                ).start()

    for j in range(n):
        pltpu.make_async_copy(
            refs[0], buffer.at[:, pl.ds(j * tokens, tokens)], sems.at[j]
        ).wait()


def weight_body(step, lhs, x_ref, out_ref, row_ref, col_ref, sum_ref):
    @pl.when(step == 0)
    def _():
        sum_ref[...] = jnp.zeros_like(sum_ref)

    unit = out_ref.shape[0]
    acc = jnp.dot(lhs, x_ref[...], preferred_element_type=f32)
    out_ref[...] = acc
    square = acc * acc
    row_ref[...] = jnp.sum(square, axis=1)[None, None, :]
    sum_ref[...] += jnp.sum(square.reshape(unit // 8, 8, square.shape[1]), axis=0)

    @pl.when(step == pl.num_programs(0) - 1)
    def _():
        col_ref[...] = jnp.sum(sum_ref[...], axis=0, keepdims=True)


def pieces_kernel(where, *refs, n):
    pieces, x_ref = refs[: 2 * n - 1], refs[2 * n - 1]
    out_ref, row_ref, col_ref, sum_ref, buffer, sems = refs[-6:]
    step = pl.program_id(0)
    unit = out_ref.shape[0]

    @pl.when(step == 0)
    def _():
        fetch(where, pieces, buffer, sems)

    start = pl.multiple_of(step * unit, unit)
    weight_body(step, buffer[pl.ds(start, unit), :], x_ref, out_ref, row_ref, col_ref, sum_ref)


def rows_kernel(lhs_ref, x_ref, *refs):
    weight_body(pl.program_id(0), lhs_ref[...], x_ref, *refs[-4:])


def weight_shapes(hidden, width, units, unit, first):
    shapes = (
        jax.ShapeDtypeStruct((hidden, width), f32),
        jax.ShapeDtypeStruct((units, 1, unit), f32),
        jax.ShapeDtypeStruct((1, width), f32),
    )
    specs = (
        pl.BlockSpec((unit, width), lambda i, *_: (i + first, 0)),
        pl.BlockSpec((1, 1, unit), lambda i, *_: (i, 0, 0)),
        pl.BlockSpec((1, width), lambda i, *_: (0, 0)),
    )
    return shapes, specs


def weight_grad_pieces(where, own, low, high, x_all, unit):
    hidden, tokens = own.shape
    n = len(low) + 1
    units = hidden // unit
    width = x_all.shape[1]
    shapes, specs = weight_shapes(hidden, width, units, unit, 0)
    grad, rows, cols = pl.pallas_call(
        functools.partial(pieces_kernel, n=n),
        out_shape=shapes,
        grid_spec=pltpu.PrefetchScalarGridSpec(
            num_scalar_prefetch=1,
            grid=(units,),
            in_specs=[pl.BlockSpec(memory_space=pl.ANY)] * (2 * n - 1)
            + [whole((n * tokens, width))],
            out_specs=specs,
            scratch_shapes=[
                pltpu.VMEM((8, width), f32),
                pltpu.VMEM((hidden, n * tokens), bf16),
                pltpu.SemaphoreType.DMA((n,)),
            ],
        ),
        name="weight_grad_pieces",
    )(where, own, *low, *high, x_all)
    return grad, rows.reshape(hidden), cols[0]


def weight_grad(lhs, x_all, unit, first, hidden, before):
    size, tokens = lhs.shape
    units = size // unit
    width = x_all.shape[1]
    shapes, specs = weight_shapes(hidden, width, units, unit, first)
    extra = [] if before is None else list(before)
    grad, rows, cols = pl.pallas_call(
        rows_kernel,
        out_shape=shapes,
        grid=(units,),
        in_specs=[
            pl.BlockSpec((unit, tokens), lambda i: (i, 0)),
            whole((tokens, width)),
        ]
        + [pl.BlockSpec(memory_space=pl.ANY) for _ in extra],
        out_specs=specs,
        scratch_shapes=[pltpu.VMEM((8, width), f32)],
        input_output_aliases={2: 0} if extra else {},
        name="weight_grad",
    )(lhs, x_all, *extra)
    return grad, rows.reshape(size), cols[0]


def input_kernel(where, lhs_ref, w_ref, *refs, last):
    acc = lax.dot_general(
        lhs_ref[...], w_ref[...], (((0,), (0,)), ((), ())), preferred_element_type=f32
    )
    if not last:
        refs[0][...] = acc
        return
    acc = acc + refs[0][...]
    mine_ref, other_ref = refs[1:]
    block = mine_ref.shape[1]
    low, high = acc[:block].astype(bf16), acc[block:].astype(bf16)
    core = where[1] % 2
    mine_ref[0] = jnp.where(core == 0, low, high)
    other_ref[0] = jnp.where(core == 0, high, low)


def input_partial(where, lhs, w_in, first_row, prev, chips):
    size, tokens = lhs.shape
    width = w_in.shape[1]
    block = tokens // chips
    if first_row % size:
        w_in, first_row = w_in[first_row : first_row + size], 0
    at = first_row // size
    row = pl.BlockSpec((block, width), lambda i, w: (i, 0))
    last = prev is not None
    piece = pl.BlockSpec((1, block // 2, width), lambda i, w: (i ^ (w[1] // 2), 0, 0))
    out = jax.ShapeDtypeStruct((chips, block // 2, width), bf16)
    return pl.pallas_call(
        functools.partial(input_kernel, last=last),
        out_shape=(out, out) if last else jax.ShapeDtypeStruct((tokens, width), f32),
        grid_spec=pltpu.PrefetchScalarGridSpec(
            num_scalar_prefetch=1,
            grid=(chips,),
            in_specs=[
                pl.BlockSpec((size, block), lambda i, w: (0, i)),
                pl.BlockSpec((size, width), lambda i, w: (at, 0)),
            ]
            + ([row] if last else []),
            out_specs=(piece, piece) if last else row,
        ),
        name="input_partial",
    )(where, lhs, w_in, *([prev] if last else []))


SPLIT = 3


def spans(units):
    cut = units - units // SPLIT
    return [(0, cut), (cut, units)]


def step(
    inputs, grad_out, pre_act, w_in, w_out, row_in_prev, col_in_prev, row_out_prev, col_out_prev
):
    n = lax.axis_size("col")
    here = lax.axis_index("col")
    where = jnp.stack([here, lax.axis_index("row")]).astype(jnp.int32)
    token_count = float(inputs.shape[0] * lax.axis_size("row"))
    hidden = w_in.shape[0]
    unit = unit_of(hidden)
    units = hidden // unit
    cuts = spans(units)

    act, slope = gelu(pre_act.T, unit, 0, units)
    low, high = line_gather(act, "col")

    grads = block_gather(grad_out)
    all_parts = []
    for a, b in cuts:
        made = hidden_partial(where, w_out, grads, n, unit, a, b - a)
        if len(made) == 4:
            grads = [made[3]]
        all_parts.append(made[:3])
    grad_all = grads[0]
    input_all = lax.all_gather(inputs, "row", axis=0, tiled=True)

    partial, before, cols_in, weighted_in, rows_in = None, None, [], [], []
    chips = lax.axis_size("row") // 2
    for p, (a, b) in enumerate(cuts):
        low_row, high_row = a * unit, b * unit
        parts, last, first = all_parts[p]
        up, down = line_scatter_sum(parts, last, first, "col")
        if p:
            up, down, _ = lax.optimization_barrier((up, down, own))
        mine = lax.dynamic_index_in_dim(parts, here, 0, keepdims=False)
        hidden_grad = mine.astype(f32) + up.astype(f32) + down.astype(f32)
        own = (hidden_grad * slope[low_row:high_row]).astype(bf16)
        pre_grad = lax.all_gather(own, "col", axis=1, tiled=True)
        partial = input_partial(where, pre_grad, w_in, low_row, partial, chips)
        grad_in, rows, cols = weight_grad(pre_grad, input_all, unit, a, hidden, before)
        rows = row_moment(total(rows, "col"), row_in_prev[low_row:high_row])
        square = grad_in[low_row:high_row]
        weighted_in.append(jnp.sum(square * square * (1.0 / rows)[:, None], axis=0))
        before = (grad_in, weighted_in[-1])
        rows_in.append(rows)
        cols_in.append(cols)

    grad_o, rows_out, cols_out = weight_grad_pieces(where, act, low, high, grad_all, unit)
    row_out = row_moment(total(rows_out, "col"), row_out_prev)
    weighted_out = jnp.sum(grad_o * grad_o * (1.0 / row_out)[:, None], axis=0)

    def finish(gradient, row_next, cols, weighted, col_prev):
        cols, weighted = total(jnp.stack([cols, weighted]), "row")
        col_next = col_moment(cols, col_prev)
        norm = jnp.sum((weighted / col_next).reshape(-1, 128), axis=0)
        norm = jnp.sum(total(norm, "col"), keepdims=True)
        rms_value = jnp.sqrt(token_count * norm / (FF * D))
        divisor = jnp.maximum(1.0, rms_value / clip_limit)
        col_scale = jnp.sqrt(token_count) / (jnp.sqrt(col_next) * divisor)
        row_scale = 1.0 / jnp.sqrt(row_next)
        col_scale, row_scale = lax.optimization_barrier((col_scale, row_scale))
        return gradient * row_scale[:, None] * col_scale[None, :], col_next

    update_out, col_out = finish(grad_o, row_out, cols_out, weighted_out, col_out_prev)
    row_in = jnp.concatenate(rows_in)
    update_in, col_in = finish(grad_in, row_in, sum(cols_in), sum(weighted_in), col_in_prev)
    input_grad = block_scatter_sum(*partial)
    return (input_grad, update_in, row_in, col_in, update_out, row_out, col_out)


def solution(mesh):
    return jax.shard_map(
        step,
        mesh=mesh,
        in_specs=(
            P("row", "col"),
            P("row", "col"),
            P("col", "row"),
            P("row", "col"),
            P("row", "col"),
            P("row"),
            P("col"),
            P("row"),
            P("col"),
        ),
        out_specs=(
            P("row", "col"),
            P("row", "col"),
            P("row"),
            P("col"),
            P("row", "col"),
            P("row"),
            P("col"),
        ),
        check_vma=False,
    )
```
